32 devices in a mesh: crop: 2 (over x), row: 8 (over z, y), col: 2 (over core).
Axes of the slice: x: 2, y: 2, z: 4, core: 2. Of those that a mesh axis runs over, the one named last changes fastest.
Arguments:
- pair_rep: bfloat16 [96, 48, 128], P(('crop', 'row'), 'col'), parts along dimension 0, may hold values from -6 to 6
- cotangent: bfloat16 [96, 48, 128], P(('crop', 'row'), 'col'), parts along dimension 0, may hold values from -6 to 6
- norm_gain: float32 [128], replicated, may hold values from 0.5 to 1.5
- norm_bias: float32 [128], replicated, may hold values from -3 to 3
- proj_weight: bfloat16 [128, 512], replicated, may hold values from -0.5 to 0.5
- gate_weight: bfloat16 [128, 128], replicated, may hold values from -0.5 to 0.5
- tri_gain: float32 [128], replicated, may hold values from 0.5 to 1.5
- tri_bias: float32 [128], replicated, may hold values from -3 to 3
- out_weight: bfloat16 [128, 128], replicated, may hold values from -0.5 to 0.5
Outputs:
- block_out: bfloat16 [96, 48, 128], P(('crop', 'row'), 'col'), parts along dimension 0
- pair_grad: float32 [96, 48, 128], P(('crop', 'row'), 'col'), parts along dimension 0
- proj_grad: float32 [256, 512], P('crop'), parts along dimension 0
- gate_grad: float32 [256, 128], P('crop'), parts along dimension 0
- out_grad: float32 [256, 128], P('crop'), parts along dimension 0
The draws below stay inside these ranges and needn't reach their ends.
There are 2 independent parts, one for each index of `crop`. The reference program is written for one: setup_inputs(seed, part) draws one part's arguments, and reference() takes and returns one part's arrays. A program takes and returns all parts, laid end to end along the dimension named above; an argument that names none is the same for every part. Nothing has to cross between parts.
All inputs are finite; a program needn't handle non-finite values.
Results may differ from the reference program's by a relative error of at most 0.0066.
Values may be sent and summed in bfloat16 or wider, within the bound.
A program may use at most 128 MiB of HBM per device.

```python
import jax
import jax.numpy as jnp
from jax import lax

C = 128
H = 128
N = 48


def block_scale(key, dims, cuts, smallest, top_value):
    def one(position, parts):
        heights = jax.random.uniform(jax.random.fold_in(jax.random.fold_in(key, 6), position), (parts,), jnp.float32, smallest / len(cuts), top_value / len(cuts))
        return jnp.repeat(jnp.exp(heights), dims[position] // parts).reshape((-1,) + (1,) * (len(dims) - position - 1))

    level = one(*cuts[0])
    for cut in cuts[1:]:
        level = level * one(*cut)
    return level


def noise(stream_key, shape, spread, most, shards=(), held_as=jnp.bfloat16):
    loudness = block_scale(stream_key, shape, shards, -0.22, 0.18) if shards else 1.0
    array = jax.random.normal(stream_key, shape, jnp.float32) * spread * loudness
    return jnp.minimum(jnp.maximum(array, -most), most).astype(held_as)


def setup_inputs(seed: int = 0, part: int = 0) -> dict:
    key_list = jax.random.split(jax.random.key(seed), 10)
    part_keys = jax.random.split(jax.random.fold_in(key_list[9], part), 10)
    pair_rep = noise(part_keys[0], (N, N, C), 1.0, 6.0, ((0, 8), (1, 2)))
    cotangent = noise(part_keys[1], (N, N, C), 1.0, 6.0, ((0, 8), (1, 2)))
    norm_gain = jnp.clip(1.0 + 0.1 * jax.random.normal(key_list[2], (C,), jnp.float32), 0.5, 1.5)
    norm_bias = noise(key_list[3], (C,), 0.5, 3.0, (), jnp.float32)
    proj_weight = noise(key_list[4], (C, 4 * H), C ** -0.5, 0.5)
    gate_weight = noise(key_list[5], (C, C), C ** -0.5, 0.5)
    tri_gain = jnp.clip(1.0 + 0.1 * jax.random.normal(key_list[6], (H,), jnp.float32), 0.5, 1.5)
    tri_bias = noise(key_list[7], (H,), 0.5, 3.0, (), jnp.float32)
    out_weight = noise(key_list[8], (H, C), H ** -0.5, 0.5)
    return dict(pair_rep=pair_rep, cotangent=cotangent, norm_gain=norm_gain, norm_bias=norm_bias, proj_weight=proj_weight, gate_weight=gate_weight, tri_gain=tri_gain, tri_bias=tri_bias, out_weight=out_weight)


def layer_norm(values, gain, bias):
    centred = values - lax.optimization_barrier(jnp.mean(values, axis=-1, keepdims=True))
    inverse = lax.rsqrt(lax.optimization_barrier(jnp.mean(centred * centred, axis=-1, keepdims=True)) + 1e-05)
    scaled = centred * inverse
    return (scaled * gain + bias, scaled, inverse)

def norm_back(grads, gain, scaled, inverse):
    weighted = grads * gain
    first = lax.optimization_barrier(jnp.mean(weighted, axis=-1, keepdims=True))
    second = lax.optimization_barrier(jnp.mean(weighted * scaled, axis=-1, keepdims=True))
    return inverse * (weighted - first - scaled * second)

def reference(pair_rep, cotangent, norm_gain, norm_bias, proj_weight, gate_weight, tri_gain, tri_bias, out_weight):
    f32 = jnp.float32
    bf16 = jnp.bfloat16
    normed_f, pair_hat, pair_inv = layer_norm(pair_rep.astype(f32), norm_gain, norm_bias)
    normed = normed_f.astype(bf16)
    flat_norm = normed.reshape(N * N, C)
    projected = jnp.dot(flat_norm, proj_weight, preferred_element_type=f32).reshape(N, N, 4 * H)
    sig_left = jax.nn.sigmoid(projected[..., 0:H])
    val_left = projected[..., H:2 * H]
    sig_right = jax.nn.sigmoid(projected[..., 2 * H:3 * H])
    val_right = projected[..., 3 * H:4 * H]
    left_edge = (sig_left * val_left).astype(bf16)
    right_edge = (sig_right * val_right).astype(bf16)
    out_gate = jax.nn.sigmoid(jnp.dot(flat_norm, gate_weight, preferred_element_type=f32).reshape(N, N, C))
    triangle = jnp.einsum('ikc,jkc->ijc', left_edge.astype(f32), right_edge.astype(f32))
    tri_f, tri_hat, tri_inv = layer_norm(triangle, tri_gain, tri_bias)
    tri_norm = tri_f.astype(bf16)
    flat_tri = tri_norm.reshape(N * N, H)
    update = jnp.dot(flat_tri, out_weight, preferred_element_type=f32).reshape(N, N, C)
    block_out = (out_gate * update).astype(bf16)
    cot = cotangent.astype(f32)
    d_update = (cot * out_gate).astype(bf16)
    d_gate = (cot * update * out_gate * (1.0 - out_gate)).astype(bf16)
    d_norm = jnp.dot(d_update.reshape(N * N, C), out_weight.T, preferred_element_type=f32).reshape(N, N, H)
    d_triangle = norm_back(d_norm, tri_gain, tri_hat, tri_inv).astype(bf16)
    d_left = jnp.einsum('ijc,jkc->ikc', d_triangle.astype(f32), right_edge.astype(f32))
    d_right = jnp.einsum('ijc,ikc->jkc', d_triangle.astype(f32), left_edge.astype(f32))
    d_proj = jnp.concatenate([d_left * val_left * sig_left * (1.0 - sig_left), d_left * sig_left, d_right * val_right * sig_right * (1.0 - sig_right), d_right * sig_right], axis=-1).astype(bf16)
    flat_dproj = d_proj.reshape(N * N, 4 * H)
    flat_dgate = d_gate.reshape(N * N, C)
    d_normed = jnp.dot(flat_dproj, proj_weight.T, preferred_element_type=f32) + jnp.dot(flat_dgate, gate_weight.T, preferred_element_type=f32)
    pair_grad = norm_back(d_normed.reshape(N, N, C), norm_gain, pair_hat, pair_inv)
    proj_grad = jnp.dot(flat_norm.T, flat_dproj, preferred_element_type=f32) / N
    gate_grad = jnp.dot(flat_norm.T, flat_dgate, preferred_element_type=f32) / N
    out_grad = jnp.dot(flat_tri.T, d_update.reshape(N * N, C), preferred_element_type=f32) / N
    return (block_out, pair_grad, proj_grad, gate_grad, out_grad)
```

```python
import functools

import jax
import jax.numpy as jnp
from jax import lax
from jax.experimental import pallas as pl
from jax.experimental.pallas import tpu as pltpu
from jax.sharding import PartitionSpec as P

F32 = jnp.float32
BF16 = jnp.bfloat16


def mean_last(values):
    return jnp.mean(values, axis=-1, keepdims=True)


def normalise(values):
    centred = values - mean_last(values)
    inverse = lax.rsqrt(mean_last(centred * centred) + 1e-05)
    return centred * inverse, inverse


def norm_back(weighted, scaled, inverse):
    return inverse * (weighted - mean_last(weighted) - scaled * mean_last(weighted * scaled))


def dot(a, b, ca=1, cb=0):
    return lax.dot_general(a, b, (((ca,), (cb,)), ((), ())), preferred_element_type=F32)


def kernel(
    R, Q, rows, K, H, C,
    x_ref, cot_ref, ng_ref, nb_ref, pw_ref, gw_ref, tg_ref, tb_ref, ow_ref,
    out_ref, pg_ref, gp_ref, gg_ref, go_ref,
    edges, right32, left32, coef, og_s, hat_s, inv_s, normed_s, dupd_s, dnorm_s,
    tri_s, tri_rcv, d32, drow, drow32, dsend, drecv, dcol32, tnorm_s, dgate_s,
    g32, gsend, grecv, gfin,
    edge_ss, edge_rs, tri_ss, tri_rs, drow_ss, drow_rs, dcol_ss, dcol_rs,
    gs_ss, gs_rs, gf_ss, gf_rs,
):
    r = lax.axis_index("row")
    q = lax.axis_index("col")
    M = rows * K
    N = rows * R
    NP = R * Q
    RPQ = R // Q
    pad = -(-rows // 8) * 8
    me = r * Q + q

    def remote(src, dst, ss, rs, rr, qq):
        return pltpu.make_async_remote_copy(
            src_ref=src, dst_ref=dst, send_sem=ss, recv_sem=rs,
            device_id={"row": rr, "col": qq}, device_id_type=pl.DeviceIdType.MESH,
        )

    def loop(lo, hi, body):
        def step(t, carry):
            body(t)
            return carry
        lax.fori_loop(lo, hi, step, 0, unroll=(hi - lo) <= 16)

    barrier = pltpu.get_barrier_semaphore()

    def greet(t):
        other = lax.rem(me + t, NP)
        pl.semaphore_signal(
            barrier, inc=1,
            device_id={"row": other // Q, "col": lax.rem(other, Q)},
            device_id_type=pl.DeviceIdType.MESH,
        )

    loop(1, NP, greet)

    hat, inv = normalise(x_ref[...].astype(F32))
    normed = (hat * ng_ref[...] + nb_ref[...]).astype(BF16)
    hat_s[...] = hat
    inv_s[...] = jnp.broadcast_to(inv, hat.shape)
    normed_s[...] = normed
    right = dot(normed, pw_ref[:, 2 * H :])
    sr = jax.nn.sigmoid(right[:, :H])
    vr = right[:, H:]
    right_edge = (sr * vr).astype(BF16)
    edges[0, r] = right_edge
    left = dot(normed, pw_ref[:, : 2 * H])
    sl = jax.nn.sigmoid(left[:, :H])
    vl = left[:, H:]
    left_edge = (sl * vl).astype(BF16)
    edges[1, r] = left_edge

    pl.semaphore_wait(barrier, NP - 1)

    for side in range(2):
        def send(t, side=side):
            other = lax.rem(r + t, R)
            remote(
                edges.at[side, r], edges.at[side, r], edge_ss.at[side, t], edge_rs.at[side, r],
                other, q,
            ).start()
        loop(1, R, send)

    def edge_wait(side):
        def wait(t):
            other = lax.rem(r + R - t, R)
            remote(
                edges.at[side, r], edges.at[side, other], edge_ss.at[side, t],
                edge_rs.at[side, other], other, q,
            ).wait_recv()
        loop(1, R, wait)

    own = pl.multiple_of(r * M, 8)
    left32[pl.ds(own, M), :] = left_edge.astype(F32)
    coef[0] = vl * sl * (1.0 - sl)
    coef[1] = sl
    coef[2] = vr * sr * (1.0 - sr)
    coef[3] = sr
    og = jax.nn.sigmoid(dot(normed, gw_ref[...]))
    og_s[...] = og
    d_update = (cot_ref[...].astype(F32) * og).astype(BF16)
    dupd_s[...] = d_update
    dnorm_s[...] = dot(d_update, ow_ref[...], 1, 1) * tg_ref[...]

    edge_wait(0)

    def widen_right(t):
        right32[pl.ds(pl.multiple_of(t * M, 8), M), :] = edges[0, t].astype(F32)
    loop(0, R, widen_right)

    def partial(half):
        base = half * (K * K)

        def step(k, accs):
            block = right32[pl.ds(base + k, K, stride=K), :]
            return tuple(
                accs[i] + left32[pl.ds(own + i * K + k, 1), :] * block for i in range(rows)
            )
        accs = lax.fori_loop(
            0, K, step, tuple(jnp.zeros((K, H), F32) for _ in range(rows)), unroll=4
        )
        for i in range(rows):
            tri_s[half, i * K : (i + 1) * K, :] = accs[i]

    for t in range(1, Q):
        other = lax.rem(q + t, Q)
        partial(other)
        remote(
            tri_s.at[other], tri_rcv.at[q], tri_ss.at[t], tri_rs.at[q], r, other
        ).start()
    partial(q)
    triangle = tri_s[q]
    for t in range(1, Q):
        other = lax.rem(q + Q - t, Q)
        remote(
            tri_s.at[other], tri_rcv.at[other], tri_ss.at[t], tri_rs.at[other], r, other
        ).wait_recv()
        triangle = triangle + tri_rcv[other]

    tri_hat, tri_inv = normalise(triangle)
    d_tri = norm_back(dnorm_s[...], tri_hat, tri_inv).astype(BF16)
    drow[q] = d_tri
    for t in range(1, Q):
        other = lax.rem(q + t, Q)
        remote(drow.at[q], drow.at[q], drow_ss.at[t], drow_rs.at[q], r, other).start()
    d_tri32 = d_tri.astype(F32)
    d32[...] = d_tri32
    for b in range(RPQ):
        parts = []
        for i in range(rows):
            piece = d32[i * K + b * rows : i * K + (b + 1) * rows, :]
            if pad > rows:
                piece = jnp.concatenate([piece, jnp.zeros((pad - rows, H), F32)], axis=0)
            parts.append(piece)
        dsend[b] = jnp.concatenate(parts, axis=0).astype(BF16)

    def each_target(act):
        for t in range(Q):
            def one(b, t=t):
                target = q * RPQ + b
                other = lax.rem(q + t, Q)
                if t:
                    act(b, t, target, other)
                else:
                    @pl.when(target != r)
                    def _():
                        act(b, t, target, other)
            loop(0, RPQ, one)

    def col_copy(b, t, target, other):
        return remote(
            dsend.at[b], drecv.at[r], dcol_ss.at[t * RPQ + b], dcol_rs.at[r], target, other
        )

    each_target(lambda b, t, target, other: col_copy(b, t, target, other).start())
    mine = r // RPQ == q

    @pl.when(mine)
    def _():
        drecv[r] = dsend[lax.rem(r, RPQ)]

    tri_norm = (tri_hat * tg_ref[...] + tb_ref[...]).astype(BF16)
    update = dot(tri_norm, ow_ref[...])
    og = og_s[...]
    out_ref[...] = (og * update).astype(BF16)
    d_gate = (cot_ref[...].astype(F32) * update * og * (1.0 - og)).astype(BF16)
    dgate_s[...] = d_gate
    g32[4 * C : 5 * C, :] = dot(normed_s[...], d_gate, 0, 0)
    g32[5 * C : 6 * C, :] = dot(tri_norm, dupd_s[...], 0, 0)

    drow32[pl.ds(pl.multiple_of(q * M, 8), M), :] = d_tri32
    for t in range(1, Q):
        other = lax.rem(q + Q - t, Q)
        remote(
            drow.at[q], drow.at[other], drow_ss.at[t], drow_rs.at[other], r, other
        ).wait_recv()
        drow32[pl.ds(pl.multiple_of(other * M, 8), M), :] = drow[other].astype(F32)

    def zeros():
        return tuple(jnp.zeros((K, H), F32) for _ in range(rows))

    accs = zeros()
    for h in range(Q):
        def left_step(j, accs, h=h):
            block = right32[pl.ds(pl.multiple_of((h * K + j) * K, 8), K), :]
            return tuple(
                accs[i] + drow32[pl.ds(h * M + i * K + j, 1), :] * block for i in range(rows)
            )
        accs = lax.fori_loop(0, K, left_step, accs, unroll=4)
    d_left = jnp.concatenate(accs, axis=0)
    d_proj = [(d_left * coef[0]).astype(BF16), (d_left * coef[1]).astype(BF16)]

    edge_wait(1)

    def widen_left(t):
        left32[pl.ds(pl.multiple_of(t * M, 8), M), :] = edges[1, t].astype(F32)
    loop(0, R, widen_left)

    owner = r // RPQ

    def col_wait(t):
        source = lax.rem(r + R - t, R)
        remote(
            dsend.at[0], drecv.at[source], dcol_ss.at[0], dcol_rs.at[source], source, owner
        ).wait_recv()
    loop(1, R, col_wait)

    @pl.when(jnp.logical_not(mine))
    def _():
        remote(dsend.at[0], drecv.at[r], dcol_ss.at[0], dcol_rs.at[r], r, owner).wait_recv()

    def widen_col(t):
        dcol32[pl.ds(pl.multiple_of(t * rows * pad, 8), rows * pad), :] = drecv[t].astype(F32)
    loop(0, R, widen_col)

    def right_step(i, accs):
        block = left32[pl.ds(pl.multiple_of(i * K, 8), K), :]
        return tuple(
            accs[j] + dcol32[pl.ds(i * pad + j, 1), :] * block for j in range(rows)
        )
    d_right = jnp.concatenate(lax.fori_loop(0, N, right_step, zeros(), unroll=4), axis=0)
    d_proj += [(d_right * coef[2]).astype(BF16), (d_right * coef[3]).astype(BF16)]

    for b in range(4):
        g32[b * C : (b + 1) * C, :] = dot(normed_s[...], d_proj[b], 0, 0)
    piece = 6 * C // NP
    for p in range(NP):
        gsend[p] = g32[p * piece : (p + 1) * piece, :].astype(BF16)

    def scatter(t):
        other = lax.rem(me + t, NP)
        return remote(
            gsend.at[other], grecv.at[me], gs_ss.at[t], gs_rs.at[me],
            other // Q, lax.rem(other, Q),
        )
    loop(1, NP, lambda t: scatter(t).start())
    grecv[me] = gsend[me]

    d_cat = jnp.concatenate(d_proj, axis=-1)
    d_normed = dot(d_cat, pw_ref[...], 1, 1) + dot(dgate_s[...], gw_ref[...], 1, 1)
    pg_ref[...] = norm_back(d_normed * ng_ref[...], hat_s[...], inv_s[...])

    def scatter_wait(t):
        other = lax.rem(me + NP - t, NP)
        remote(
            gsend.at[0], grecv.at[other], gs_ss.at[t], gs_rs.at[other],
            other // Q, lax.rem(other, Q),
        ).wait_recv()
    loop(1, NP, scatter_wait)
    total = grecv[0].astype(F32)
    for p in range(1, NP):
        total = total + grecv[p].astype(F32)
    gfin[me] = (total / N).astype(BF16)

    def spread(t):
        other = lax.rem(me + t, NP)
        return remote(
            gfin.at[me], gfin.at[me], gf_ss.at[t], gf_rs.at[me],
            other // Q, lax.rem(other, Q),
        )
    loop(1, NP, lambda t: spread(t).start())

    for side in range(2):
        loop(1, R, lambda t, side=side: remote(
            edges.at[side, r], edges.at[side, r], edge_ss.at[side, t], edge_rs.at[side, r], r, q
        ).wait_send())
    for t in range(1, Q):
        other = lax.rem(q + t, Q)
        remote(tri_s.at[other], tri_rcv.at[q], tri_ss.at[t], tri_rs.at[q], r, other).wait_send()
        remote(drow.at[q], drow.at[q], drow_ss.at[t], drow_rs.at[q], r, other).wait_send()
    each_target(lambda b, t, target, other: col_copy(b, t, target, other).wait_send())
    loop(1, NP, lambda t: scatter(t).wait_send())

    def spread_wait(t):
        other = lax.rem(me + NP - t, NP)
        remote(
            gfin.at[me], gfin.at[other], gf_ss.at[t], gf_rs.at[other],
            other // Q, lax.rem(other, Q),
        ).wait_recv()
    loop(1, NP, spread_wait)
    for p in range(NP):
        g32[p * piece : (p + 1) * piece, :] = gfin[p].astype(F32)
    for b in range(4):
        gp_ref[:, b * H : (b + 1) * H] = g32[b * C : (b + 1) * C, :]
    gg_ref[...] = g32[4 * C : 5 * C, :]
    go_ref[...] = g32[5 * C : 6 * C, :]
    loop(1, NP, lambda t: spread(t).wait_send())


def local(R, Q, pair_rep, cotangent, ng, nb, pw, gw, tg, tb, ow):
    rows, K, C = pair_rep.shape
    H = tg.shape[0]
    M = rows * K
    NP = R * Q
    RPQ = R // Q
    pad = -(-rows // 8) * 8
    piece = 6 * C // NP
    dma = pltpu.SemaphoreType.DMA
    vmem = pltpu.VMEM
    spec = pl.BlockSpec(memory_space=pltpu.VMEM)
    shapes = (
        jax.ShapeDtypeStruct((M, C), BF16),
        jax.ShapeDtypeStruct((M, C), F32),
        jax.ShapeDtypeStruct((C, 4 * H), F32),
        jax.ShapeDtypeStruct((C, C), F32),
        jax.ShapeDtypeStruct((H, C), F32),
    )
    outs = pl.pallas_call(
        functools.partial(kernel, R, Q, rows, K, H, C),
        out_shape=shapes,
        in_specs=[spec] * 9,
        out_specs=[spec] * 5,
        scratch_shapes=[
            vmem((2, R, M, H), BF16),
            vmem((R * M, H), F32),
            vmem((R * M, H), F32),
            vmem((4, M, H), F32),
            vmem((M, C), F32),
            vmem((M, C), F32),
            vmem((M, C), F32),
            vmem((M, C), BF16),
            vmem((M, C), BF16),
            vmem((M, H), F32),
            vmem((Q, M, H), F32),
            vmem((Q, M, H), F32),
            vmem((M, H), F32),
            vmem((Q, M, H), BF16),
            vmem((Q * M, H), F32),
            vmem((RPQ, rows * pad, H), BF16),
            vmem((R, rows * pad, H), BF16),
            vmem((R * rows * pad, H), F32),
            vmem((M, H), BF16),
            vmem((M, C), BF16),
            vmem((6 * C, H), F32),
            vmem((NP, piece, H), BF16),
            vmem((NP, piece, H), BF16),
            vmem((NP, piece, H), BF16),
            dma((2, R)), dma((2, R)),
            dma((Q,)), dma((Q,)),
            dma((Q,)), dma((Q,)),
            dma((R,)), dma((R,)),
            dma((NP,)), dma((NP,)),
            dma((NP,)), dma((NP,)),
        ],
        compiler_params=pltpu.CompilerParams(
            collective_id=0, has_side_effects=True, vmem_limit_bytes=60 * 1024 * 1024
        ),
        name="triangle_step",
    )(
        pair_rep.reshape(M, C), cotangent.reshape(M, C), ng.reshape(1, C), nb.reshape(1, C),
        pw, gw, tg.reshape(1, H), tb.reshape(1, H), ow,
    )
    return (
        outs[0].reshape(rows, K, C), outs[1].reshape(rows, K, C), outs[2], outs[3], outs[4],
    )


def solution(mesh):
    tile = P(("crop", "row"), "col", None)
    grad = P("crop", None)
    return jax.shard_map(
        functools.partial(local, mesh.shape["row"], mesh.shape["col"]),
        mesh=mesh,
        in_specs=(tile, tile, P(), P(), P(), P(), P(), P(), P()),
        out_specs=(tile, tile, grad, grad, grad),
        check_vma=False,
    )
```

```python
import functools

import jax
import jax.numpy as jnp
from jax import lax
from jax.experimental import pallas as pl
from jax.experimental.pallas import tpu as pltpu
from jax.sharding import PartitionSpec as P

F32 = jnp.float32
BF16 = jnp.bfloat16


def mean_last(values):
    return jnp.mean(values, axis=-1, keepdims=True)


def normalise(values):
    centred = values - mean_last(values)
    inverse = lax.rsqrt(mean_last(centred * centred) + 1e-05)
    return centred * inverse, inverse


def norm_back(weighted, scaled, inverse):
    return inverse * (weighted - mean_last(weighted) - scaled * mean_last(weighted * scaled))


def dot(a, b, ca=1, cb=0):
    return lax.dot_general(a, b, (((ca,), (cb,)), ((), ())), preferred_element_type=F32)


def kernel(
    R, Q, rows, K, H, C,
    x_ref, cot_ref, ng_ref, nb_ref, pw_ref, gw_ref, tg_ref, tb_ref, ow_ref,
    out_ref, pg_ref, gall_ref,
    edges, right32, left32, coef, og_s, hat_s, inv_s, normed_s, dupd_s, dnorm_s,
    tri_s, tri_rcv, d32, drow, drow32, dsend, drecv, dcol32, tnorm_s, dgate_s,
    gsend, grecv, gfin,
    edge_ss, edge_rs, tri_ss, tri_rs, drow_ss, drow_rs, dcol_ss, dcol_rs,
    gs_ss, gs_rs, gf_ss, gf_rs,
):
    r = lax.axis_index("row")
    q = lax.axis_index("col")
    M = rows * K
    N = rows * R
    NP = R * Q
    RPQ = R // Q
    pad = -(-rows // 8) * 8
    me = r * Q + q

    def remote(src, dst, ss, rs, rr, qq):
        return pltpu.make_async_remote_copy(
            src_ref=src, dst_ref=dst, send_sem=ss, recv_sem=rs,
            device_id={"row": rr, "col": qq}, device_id_type=pl.DeviceIdType.MESH,
        )

    def loop(lo, hi, body):
        def step(t, carry):
            body(t)
            return carry
        lax.fori_loop(lo, hi, step, 0, unroll=(hi - lo) <= 16)

    barrier = pltpu.get_barrier_semaphore()

    def greet(t):
        other = lax.rem(me + t, NP)
        pl.semaphore_signal(
            barrier, inc=1,
            device_id={"row": other // Q, "col": lax.rem(other, Q)},
            device_id_type=pl.DeviceIdType.MESH,
        )

    loop(1, NP, greet)

    piece = 2 * C // NP
    per = NP // 2

    def scatter(g, t):
        other = lax.rem(me + t, NP)
        return remote(
            gsend.at[g, other], grecv.at[g, me], gs_ss.at[g, t], gs_rs.at[g, me],
            other // Q, lax.rem(other, Q),
        )

    def scatter_start(g, first, second):
        for p in range(per):
            gsend[g, p] = first[p * piece : (p + 1) * piece, :].astype(BF16)
            gsend[g, per + p] = second[p * piece : (p + 1) * piece, :].astype(BF16)
        loop(1, NP, lambda t: scatter(g, t).start())
        grecv[g, me] = gsend[g, me]

    def spread(g, t):
        other = lax.rem(me + t, NP)
        return remote(
            gfin.at[g, me], gfin.at[g, me], gf_ss.at[g, t], gf_rs.at[g, me],
            other // Q, lax.rem(other, Q),
        )

    def spread_start(g):
        def wait(t):
            other = lax.rem(me + NP - t, NP)
            remote(
                gsend.at[g, 0], grecv.at[g, other], gs_ss.at[g, t], gs_rs.at[g, other],
                other // Q, lax.rem(other, Q),
            ).wait_recv()
        loop(1, NP, wait)
        total = grecv[g, 0].astype(F32)
        for p in range(1, NP):
            total = total + grecv[g, p].astype(F32)
        gfin[g, me] = (total / N).astype(BF16)
        loop(1, NP, lambda t: spread(g, t).start())

    def spread_wait(g, t):
        other = lax.rem(me + NP - t, NP)
        remote(
            gfin.at[g, me], gfin.at[g, other], gf_ss.at[g, t], gf_rs.at[g, other],
            other // Q, lax.rem(other, Q),
        ).wait_recv()

    hat, inv = normalise(x_ref[...].astype(F32))
    normed = (hat * ng_ref[...] + nb_ref[...]).astype(BF16)
    hat_s[...] = hat
    inv_s[...] = jnp.broadcast_to(inv, hat.shape)
    normed_s[...] = normed
    right = dot(normed, pw_ref[:, 2 * H :])
    sr = jax.nn.sigmoid(right[:, :H])
    vr = right[:, H:]
    right_edge = (sr * vr).astype(BF16)
    edges[0, r] = right_edge
    left = dot(normed, pw_ref[:, : 2 * H])
    sl = jax.nn.sigmoid(left[:, :H])
    vl = left[:, H:]
    left_edge = (sl * vl).astype(BF16)
    edges[1, r] = left_edge

    pl.semaphore_wait(barrier, NP - 1)

    for side in range(2):
        def send(t, side=side):
            other = lax.rem(r + t, R)
            remote(
                edges.at[side, r], edges.at[side, r], edge_ss.at[side, t], edge_rs.at[side, r],
                other, q,
            ).start()
        loop(1, R, send)

    def edge_wait(side):
        def wait(t):
            other = lax.rem(r + R - t, R)
            remote(
                edges.at[side, r], edges.at[side, other], edge_ss.at[side, t],
                edge_rs.at[side, other], other, q,
            ).wait_recv()
        loop(1, R, wait)

    own = pl.multiple_of(r * M, 8)
    left32[pl.ds(own, M), :] = left_edge.astype(F32)
    coef[0] = vl * sl * (1.0 - sl)
    coef[1] = sl
    coef[2] = vr * sr * (1.0 - sr)
    coef[3] = sr
    og = jax.nn.sigmoid(dot(normed, gw_ref[...]))
    og_s[...] = og
    d_update = (cot_ref[...].astype(F32) * og).astype(BF16)
    dupd_s[...] = d_update
    dnorm_s[...] = dot(d_update, ow_ref[...], 1, 1) * tg_ref[...]

    edge_wait(0)

    def widen_right(t):
        right32[pl.ds(pl.multiple_of(t * M, 8), M), :] = edges[0, t].astype(F32)
    loop(0, R, widen_right)

    def partial(half):
        base = half * (K * K)

        def step(k, accs):
            block = right32[pl.ds(base + k, K, stride=K), :]
            return tuple(
                accs[i] + left32[pl.ds(own + i * K + k, 1), :] * block for i in range(rows)
            )
        accs = lax.fori_loop(
            0, K, step, tuple(jnp.zeros((K, H), F32) for _ in range(rows)), unroll=4
        )
        for i in range(rows):
            tri_s[half, i * K : (i + 1) * K, :] = accs[i]

    for t in range(1, Q):
        other = lax.rem(q + t, Q)
        partial(other)
        remote(
            tri_s.at[other], tri_rcv.at[q], tri_ss.at[t], tri_rs.at[q], r, other
        ).start()
    partial(q)
    triangle = tri_s[q]
    for t in range(1, Q):
        other = lax.rem(q + Q - t, Q)
        remote(
            tri_s.at[other], tri_rcv.at[other], tri_ss.at[t], tri_rs.at[other], r, other
        ).wait_recv()
        triangle = triangle + tri_rcv[other]

    tri_hat, tri_inv = normalise(triangle)
    d_tri = norm_back(dnorm_s[...], tri_hat, tri_inv).astype(BF16)
    drow[q] = d_tri
    for t in range(1, Q):
        other = lax.rem(q + t, Q)
        remote(drow.at[q], drow.at[q], drow_ss.at[t], drow_rs.at[q], r, other).start()
    d_tri32 = d_tri.astype(F32)
    d32[...] = d_tri32
    for b in range(RPQ):
        parts = []
        for i in range(rows):
            block = d32[i * K + b * rows : i * K + (b + 1) * rows, :]
            if pad > rows:
                block = jnp.concatenate([block, jnp.zeros((pad - rows, H), F32)], axis=0)
            parts.append(block)
        dsend[b] = jnp.concatenate(parts, axis=0).astype(BF16)

    def each_target(act):
        for t in range(Q):
            def one(b, t=t):
                target = q * RPQ + b
                other = lax.rem(q + t, Q)
                if t:
                    act(b, t, target, other)
                else:
                    @pl.when(target != r)
                    def _():
                        act(b, t, target, other)
            loop(0, RPQ, one)

    def col_copy(b, t, target, other):
        return remote(
            dsend.at[b], drecv.at[r], dcol_ss.at[t * RPQ + b], dcol_rs.at[r], target, other
        )

    each_target(lambda b, t, target, other: col_copy(b, t, target, other).start())
    mine = r // RPQ == q

    @pl.when(mine)
    def _():
        drecv[r] = dsend[lax.rem(r, RPQ)]

    tri_norm = (tri_hat * tg_ref[...] + tb_ref[...]).astype(BF16)
    update = dot(tri_norm, ow_ref[...])
    og = og_s[...]
    out_ref[...] = (og * update).astype(BF16)
    d_gate = (cot_ref[...].astype(F32) * update * og * (1.0 - og)).astype(BF16)
    dgate_s[...] = d_gate
    scatter_start(0, dot(normed_s[...], d_gate, 0, 0), dot(tri_norm, dupd_s[...], 0, 0))

    drow32[pl.ds(pl.multiple_of(q * M, 8), M), :] = d_tri32
    for t in range(1, Q):
        other = lax.rem(q + Q - t, Q)
        remote(
            drow.at[q], drow.at[other], drow_ss.at[t], drow_rs.at[other], r, other
        ).wait_recv()
        drow32[pl.ds(pl.multiple_of(other * M, 8), M), :] = drow[other].astype(F32)

    def zeros():
        return tuple(jnp.zeros((K, H), F32) for _ in range(rows))

    accs = zeros()
    for h in range(Q):
        def left_step(j, accs, h=h):
            block = right32[pl.ds(pl.multiple_of((h * K + j) * K, 8), K), :]
            return tuple(
                accs[i] + drow32[pl.ds(h * M + i * K + j, 1), :] * block for i in range(rows)
            )
        accs = lax.fori_loop(0, K, left_step, accs, unroll=4)
    d_left = jnp.concatenate(accs, axis=0)
    d_proj = [(d_left * coef[0]).astype(BF16), (d_left * coef[1]).astype(BF16)]
    scatter_start(1, dot(normed_s[...], d_proj[0], 0, 0), dot(normed_s[...], d_proj[1], 0, 0))

    edge_wait(1)

    def widen_left(t):
        left32[pl.ds(pl.multiple_of(t * M, 8), M), :] = edges[1, t].astype(F32)
    loop(0, R, widen_left)

    owner = r // RPQ

    def col_wait(t):
        source = lax.rem(r + R - t, R)
        remote(
            dsend.at[0], drecv.at[source], dcol_ss.at[0], dcol_rs.at[source], source, owner
        ).wait_recv()
    loop(1, R, col_wait)

    @pl.when(jnp.logical_not(mine))
    def _():
        remote(dsend.at[0], drecv.at[r], dcol_ss.at[0], dcol_rs.at[r], r, owner).wait_recv()

    def widen_col(t):
        dcol32[pl.ds(pl.multiple_of(t * rows * pad, 8), rows * pad), :] = drecv[t].astype(F32)
    loop(0, R, widen_col)

    def right_step(i, accs):
        block = left32[pl.ds(pl.multiple_of(i * K, 8), K), :]
        return tuple(
            accs[j] + dcol32[pl.ds(i * pad + j, 1), :] * block for j in range(rows)
        )
    d_right = jnp.concatenate(lax.fori_loop(0, N, right_step, zeros(), unroll=4), axis=0)
    d_proj += [(d_right * coef[2]).astype(BF16), (d_right * coef[3]).astype(BF16)]

    scatter_start(2, dot(normed_s[...], d_proj[2], 0, 0), dot(normed_s[...], d_proj[3], 0, 0))
    spread_start(0)
    spread_start(1)

    d_cat = jnp.concatenate(d_proj, axis=-1)
    d_normed = dot(d_cat, pw_ref[...], 1, 1) + dot(dgate_s[...], gw_ref[...], 1, 1)
    pg_ref[...] = norm_back(d_normed * ng_ref[...], hat_s[...], inv_s[...])

    spread_start(2)

    for side in range(2):
        loop(1, R, lambda t, side=side: remote(
            edges.at[side, r], edges.at[side, r], edge_ss.at[side, t], edge_rs.at[side, r], r, q
        ).wait_send())
    for t in range(1, Q):
        other = lax.rem(q + t, Q)
        remote(tri_s.at[other], tri_rcv.at[q], tri_ss.at[t], tri_rs.at[q], r, other).wait_send()
        remote(drow.at[q], drow.at[q], drow_ss.at[t], drow_rs.at[q], r, other).wait_send()
    each_target(lambda b, t, target, other: col_copy(b, t, target, other).wait_send())
    for g in range(3):
        loop(1, NP, lambda t, g=g: scatter(g, t).wait_send())
        loop(1, NP, lambda t, g=g: spread_wait(g, t))
    gall_ref[...] = gfin[...]
    for g in range(3):
        loop(1, NP, lambda t, g=g: spread(g, t).wait_send())


def finish(NP, piece, C, H, block_ref, grad_ref, gall_ref, out_ref, pg_ref, gp_ref, gg_ref, go_ref):
    out_ref[...] = block_ref[...]
    pg_ref[...] = grad_ref[...]
    targets = (
        (gg_ref, 0), (go_ref, 0), (gp_ref, 0), (gp_ref, H), (gp_ref, 2 * H), (gp_ref, 3 * H),
    )
    per = C // piece
    for t, (ref, col) in enumerate(targets):
        for p in range(per):
            whole = (t % 2) * per + p
            ref[p * piece : (p + 1) * piece, col : col + H] = gall_ref[t // 2, whole].astype(F32)


def local(R, Q, pair_rep, cotangent, ng, nb, pw, gw, tg, tb, ow):
    rows, K, C = pair_rep.shape
    H = tg.shape[0]
    M = rows * K
    NP = R * Q
    RPQ = R // Q
    pad = -(-rows // 8) * 8
    piece = 2 * C // NP
    dma = pltpu.SemaphoreType.DMA
    vmem = pltpu.VMEM
    spec = pl.BlockSpec(memory_space=pltpu.VMEM)
    shapes = (
        jax.ShapeDtypeStruct((M, C), BF16),
        jax.ShapeDtypeStruct((M, C), F32),
        jax.ShapeDtypeStruct((3, NP, piece, H), BF16),
    )
    parts = pl.pallas_call(
        functools.partial(kernel, R, Q, rows, K, H, C),
        out_shape=shapes,
        in_specs=[spec] * 9,
        out_specs=[spec] * 3,
        scratch_shapes=[
            vmem((2, R, M, H), BF16),
            vmem((R * M, H), F32),
            vmem((R * M, H), F32),
            vmem((4, M, H), F32),
            vmem((M, C), F32),
            vmem((M, C), F32),
            vmem((M, C), F32),
            vmem((M, C), BF16),
            vmem((M, C), BF16),
            vmem((M, H), F32),
            vmem((Q, M, H), F32),
            vmem((Q, M, H), F32),
            vmem((M, H), F32),
            vmem((Q, M, H), BF16),
            vmem((Q * M, H), F32),
            vmem((RPQ, rows * pad, H), BF16),
            vmem((R, rows * pad, H), BF16),
            vmem((R * rows * pad, H), F32),
            vmem((M, H), BF16),
            vmem((M, C), BF16),
            vmem((3, NP, piece, H), BF16),
            vmem((3, NP, piece, H), BF16),
            vmem((3, NP, piece, H), BF16),
            dma((2, R)), dma((2, R)),
            dma((Q,)), dma((Q,)),
            dma((Q,)), dma((Q,)),
            dma((R,)), dma((R,)),
            dma((3, NP)), dma((3, NP)),
            dma((3, NP)), dma((3, NP)),
        ],
        compiler_params=pltpu.CompilerParams(
            collective_id=0, has_side_effects=True, vmem_limit_bytes=60 * 1024 * 1024
        ),
        name="triangle_step",
    )(
        pair_rep.reshape(M, C), cotangent.reshape(M, C), ng.reshape(1, C), nb.reshape(1, C),
        pw, gw, tg.reshape(1, H), tb.reshape(1, H), ow,
    )
    outs = pl.pallas_call(
        functools.partial(finish, NP, piece, C, H),
        out_shape=(
            shapes[0],
            shapes[1],
            jax.ShapeDtypeStruct((C, 4 * H), F32),
            jax.ShapeDtypeStruct((C, C), F32),
            jax.ShapeDtypeStruct((H, C), F32),
        ),
        in_specs=[spec] * 3,
        out_specs=[spec] * 5,
        name="finish",
    )(*parts)
    return (
        outs[0].reshape(rows, K, C), outs[1].reshape(rows, K, C), outs[2], outs[3], outs[4],
    )


def solution(mesh):
    tile = P(("crop", "row"), "col", None)
    grad = P("crop", None)
    return jax.shard_map(
        functools.partial(local, mesh.shape["row"], mesh.shape["col"]),
        mesh=mesh,
        in_specs=(tile, tile, P(), P(), P(), P(), P(), P(), P()),
        out_specs=(tile, tile, grad, grad, grad),
        check_vma=False,
    )
```

```python
import functools

import jax
import jax.numpy as jnp
from jax import lax
from jax.experimental import pallas as pl
from jax.experimental.pallas import tpu as pltpu
from jax.sharding import PartitionSpec as P

F32 = jnp.float32
BF16 = jnp.bfloat16


def mean_last(values):
    return jnp.mean(values, axis=-1, keepdims=True)


def normalise(values):
    centred = values - mean_last(values)
    inverse = lax.rsqrt(mean_last(centred * centred) + 1e-05)
    return centred * inverse, inverse


def norm_back(weighted, scaled, inverse):
    return inverse * (weighted - mean_last(weighted) - scaled * mean_last(weighted * scaled))


def dot(a, b, ca=1, cb=0):
    return lax.dot_general(a, b, (((ca,), (cb,)), ((), ())), preferred_element_type=F32)


def kernel(
    R, Q, rows, K, H, C,
    x_ref, cot_ref, ng_ref, nb_ref, pw_ref, gw_ref, tg_ref, tb_ref, ow_ref,
    out_ref, pg_ref, gall_ref,
    edges, right32, left32, coef, og_s, hat_s, inv_s, normed_s, dupd_s, dnorm_s,
    tri_s, tri_rcv, d32, drow, drow32, dsend, drecv, dcol32, tnorm_s, dgate_s,
    gsend, grecv, gfin,
    edge_ss, edge_rs, tri_ss, tri_rs, drow_ss, drow_rs, dcol_ss, dcol_rs,
    gs_ss, gs_rs, gf_ss, gf_rs,
):
    r = lax.axis_index("row")
    q = lax.axis_index("col")
    M = rows * K
    N = rows * R
    NP = R * Q
    RPQ = R // Q
    pad = -(-rows // 8) * 8
    me = r * Q + q

    def remote(src, dst, ss, rs, rr, qq):
        return pltpu.make_async_remote_copy(
            src_ref=src, dst_ref=dst, send_sem=ss, recv_sem=rs,
            device_id={"row": rr, "col": qq}, device_id_type=pl.DeviceIdType.MESH,
        )

    def loop(lo, hi, body):
        if hi - lo <= 16:
            for t in range(lo, hi):
                body(t)
            return

        def step(t, carry):
            body(t)
            return carry
        lax.fori_loop(lo, hi, step, 0)

    def wrap(value, size):
        return jnp.where(value >= size, value - size, value)

    def peer(t):
        rr, qq = wrap(r + t // Q, R), wrap(q + t % Q, Q)
        return rr, qq, rr * Q + qq

    barrier = pltpu.get_barrier_semaphore()

    def greet(t):
        rr, qq, _ = peer(t)
        pl.semaphore_signal(
            barrier, inc=1,
            device_id={"row": rr, "col": qq},
            device_id_type=pl.DeviceIdType.MESH,
        )

    loop(1, NP, greet)

    piece = 2 * C // NP
    per = NP // 2

    def scatter(g, t):
        rr, qq, other = peer(t)
        return remote(
            gsend.at[g, other], grecv.at[g, me], gs_ss.at[g], gs_rs.at[g], rr, qq
        )

    def scatter_all(g):
        block = pl.ds(0, NP - 1)
        return remote(
            gsend.at[g, block], grecv.at[g, block], gs_ss.at[g], gs_rs.at[g], r, q
        )

    def scatter_start(g, first, second):
        for p in range(per):
            gsend[g, p] = first[p * piece : (p + 1) * piece, :].astype(BF16)
            gsend[g, per + p] = second[p * piece : (p + 1) * piece, :].astype(BF16)
        loop(1, NP, lambda t: scatter(g, t).start())
        grecv[g, me] = gsend[g, me]

    def spread(g, t):
        rr, qq, _ = peer(t)
        return remote(gfin.at[g, me], gfin.at[g, me], gf_ss.at[g], gf_rs.at[g], rr, qq)

    def spread_all(g):
        block = pl.ds(0, NP - 1)
        return remote(gfin.at[g, block], gfin.at[g, block], gf_ss.at[g], gf_rs.at[g], r, q)

    def spread_start(g):
        scatter_all(g).wait_recv()
        total = grecv[g, 0].astype(F32)
        for p in range(1, NP):
            total = total + grecv[g, p].astype(F32)
        gfin[g, me] = (total / N).astype(BF16)
        loop(1, NP, lambda t: spread(g, t).start())

    hat, inv = normalise(x_ref[...].astype(F32))
    normed = (hat * ng_ref[...] + nb_ref[...]).astype(BF16)
    hat_s[...] = hat
    inv_s[...] = jnp.broadcast_to(inv, hat.shape)
    normed_s[...] = normed
    right = dot(normed, pw_ref[:, 2 * H :])
    sr = jax.nn.sigmoid(right[:, :H])
    vr = right[:, H:]
    right_edge = (sr * vr).astype(BF16)
    edges[0, r] = right_edge
    left = dot(normed, pw_ref[:, : 2 * H])
    sl = jax.nn.sigmoid(left[:, :H])
    vl = left[:, H:]
    left_edge = (sl * vl).astype(BF16)
    edges[1, r] = left_edge

    pl.semaphore_wait(barrier, NP - 1)

    B = 2 if R % 2 == 0 else 1
    A = R // B
    place, lane = r // B, lax.rem(r, B)

    def along(act):
        for d in range(1, A):
            for spot in (place - d, place + d):
                @pl.when(jnp.logical_and(spot >= 0, spot < A))
                def _(spot=spot):
                    act(jnp.clip(spot, 0, A - 1))

    def line_copy(side, spot):
        return remote(
            edges.at[side, r], edges.at[side, r], edge_ss.at[side, spot],
            edge_rs.at[side, r], spot * B + lane, q,
        )

    def lane_copy(side, spot):
        slot = spot * B + lane
        return remote(
            edges.at[side, slot], edges.at[side, slot], edge_ss.at[side, A + spot],
            edge_rs.at[side, slot], place * B + (B - 1 - lane), q,
        )

    def edge_send(side):
        along(lambda spot: line_copy(side, spot).start())
        if B > 1:
            lane_copy(side, place).start()

    def edge_pass(side):
        def one(spot):
            slot = spot * B + lane
            remote(
                edges.at[side, r], edges.at[side, slot], edge_ss.at[side, 0],
                edge_rs.at[side, slot], slot, q,
            ).wait_recv()
            if B > 1:
                lane_copy(side, spot).start()
        along(one)

    def edge_wait(side):
        if B > 1:
            def wait(spot):
                slot = spot * B + (B - 1 - lane)
                remote(
                    edges.at[side, r], edges.at[side, slot], edge_ss.at[side, 0],
                    edge_rs.at[side, slot], place * B + (B - 1 - lane), q,
                ).wait_recv()
            loop(0, A, wait)

    edge_send(0)
    edge_send(1)

    own = pl.multiple_of(r * M, 8)
    left32[pl.ds(own, M), :] = left_edge.astype(F32)
    coef[0] = vl * sl * (1.0 - sl)
    coef[1] = sl
    coef[2] = vr * sr * (1.0 - sr)
    coef[3] = sr
    og = jax.nn.sigmoid(dot(normed, gw_ref[...]))
    og_s[...] = og
    d_update = (cot_ref[...].astype(F32) * og).astype(BF16)
    dupd_s[...] = d_update
    dnorm_s[...] = dot(d_update, ow_ref[...], 1, 1) * tg_ref[...]

    edge_pass(0)
    edge_wait(0)

    def widen_right(t):
        right32[pl.ds(pl.multiple_of(t * M, 8), M), :] = edges[0, t].astype(F32)
    loop(0, R, widen_right)

    def partial(half):
        base = half * (K * K)

        def step(k, accs):
            block = right32[pl.ds(base + k, K, stride=K), :]
            return tuple(
                accs[i] + left32[pl.ds(own + i * K + k, 1), :] * block for i in range(rows)
            )
        accs = lax.fori_loop(
            0, K, step, tuple(jnp.zeros((K, H), F32) for _ in range(rows)), unroll=4
        )
        for i in range(rows):
            tri_s[half, i * K : (i + 1) * K, :] = accs[i]

    for t in range(1, Q):
        other = wrap(q + t, Q)
        partial(other)
        remote(
            tri_s.at[other], tri_rcv.at[q], tri_ss.at[t], tri_rs.at[q], r, other
        ).start()
    partial(q)
    edge_pass(1)
    triangle = tri_s[q]
    for t in range(1, Q):
        other = wrap(q + Q - t, Q)
        remote(
            tri_s.at[other], tri_rcv.at[other], tri_ss.at[t], tri_rs.at[other], r, other
        ).wait_recv()
        triangle = triangle + tri_rcv[other]

    tri_hat, tri_inv = normalise(triangle)
    d_tri = norm_back(dnorm_s[...], tri_hat, tri_inv).astype(BF16)
    drow[q] = d_tri
    for t in range(1, Q):
        other = wrap(q + t, Q)
        remote(drow.at[q], drow.at[q], drow_ss.at[t], drow_rs.at[q], r, other).start()
    d_tri32 = d_tri.astype(F32)
    d32[...] = d_tri32
    for b in range(RPQ):
        parts = []
        for i in range(rows):
            block = d32[i * K + b * rows : i * K + (b + 1) * rows, :]
            if pad > rows:
                block = jnp.concatenate([block, jnp.zeros((pad - rows, H), F32)], axis=0)
            parts.append(block)
        dsend[b] = jnp.concatenate(parts, axis=0).astype(BF16)

    def each_target(act):
        for t in range(Q):
            def one(b, t=t):
                target = q * RPQ + b
                other = wrap(q + t, Q)
                if t:
                    act(b, t, target, other)
                else:
                    @pl.when(target != r)
                    def _():
                        act(b, t, target, other)
            loop(0, RPQ, one)

    def col_copy(b, t, target, other):
        return remote(
            dsend.at[b], drecv.at[r], dcol_ss.at[t * RPQ + b], dcol_rs.at[r], target, other
        )

    each_target(lambda b, t, target, other: col_copy(b, t, target, other).start())
    mine = r // RPQ == q

    @pl.when(mine)
    def _():
        drecv[r] = dsend[lax.rem(r, RPQ)]

    tri_norm = (tri_hat * tg_ref[...] + tb_ref[...]).astype(BF16)
    update = dot(tri_norm, ow_ref[...])
    og = og_s[...]
    out_ref[...] = (og * update).astype(BF16)
    d_gate = (cot_ref[...].astype(F32) * update * og * (1.0 - og)).astype(BF16)
    dgate_s[...] = d_gate
    scatter_start(0, dot(normed_s[...], d_gate, 0, 0), dot(tri_norm, dupd_s[...], 0, 0))

    drow32[pl.ds(pl.multiple_of(q * M, 8), M), :] = d_tri32
    for t in range(1, Q):
        other = wrap(q + Q - t, Q)
        remote(
            drow.at[q], drow.at[other], drow_ss.at[t], drow_rs.at[other], r, other
        ).wait_recv()
        drow32[pl.ds(pl.multiple_of(other * M, 8), M), :] = drow[other].astype(F32)

    def zeros():
        return tuple(jnp.zeros((K, H), F32) for _ in range(rows))

    accs = zeros()
    for h in range(Q):
        def left_step(j, accs, h=h):
            block = right32[pl.ds(pl.multiple_of((h * K + j) * K, 8), K), :]
            return tuple(
                accs[i] + drow32[pl.ds(h * M + i * K + j, 1), :] * block for i in range(rows)
            )
        accs = lax.fori_loop(0, K, left_step, accs, unroll=4)
    d_left = jnp.concatenate(accs, axis=0)
    d_proj = [(d_left * coef[0]).astype(BF16), (d_left * coef[1]).astype(BF16)]
    wide = dot(normed_s[...], jnp.concatenate(d_proj, axis=-1), 0, 0)
    scatter_start(1, wide[:, :H], wide[:, H:])

    edge_wait(1)

    def widen_left(t):
        left32[pl.ds(pl.multiple_of(t * M, 8), M), :] = edges[1, t].astype(F32)
    loop(0, R, widen_left)

    owner = r // RPQ

    def col_wait(t):
        source = wrap(r + R - t, R)
        remote(
            dsend.at[0], drecv.at[source], dcol_ss.at[0], dcol_rs.at[source], source, owner
        ).wait_recv()
    loop(1, R, col_wait)

    @pl.when(jnp.logical_not(mine))
    def _():
        remote(dsend.at[0], drecv.at[r], dcol_ss.at[0], dcol_rs.at[r], r, owner).wait_recv()

    def widen_col(t):
        dcol32[pl.ds(pl.multiple_of(t * rows * pad, 8), rows * pad), :] = drecv[t].astype(F32)
    loop(0, R, widen_col)

    def right_step(i, accs):
        block = left32[pl.ds(pl.multiple_of(i * K, 8), K), :]
        return tuple(
            accs[j] + dcol32[pl.ds(i * pad + j, 1), :] * block for j in range(rows)
        )
    d_right = jnp.concatenate(lax.fori_loop(0, N, right_step, zeros(), unroll=4), axis=0)
    d_proj += [(d_right * coef[2]).astype(BF16), (d_right * coef[3]).astype(BF16)]

    wide = dot(normed_s[...], jnp.concatenate(d_proj[2:], axis=-1), 0, 0)
    scatter_start(2, wide[:, :H], wide[:, H:])
    spread_start(0)
    spread_start(1)

    d_cat = jnp.concatenate(d_proj, axis=-1)
    d_normed = dot(d_cat, pw_ref[...], 1, 1) + dot(dgate_s[...], gw_ref[...], 1, 1)
    pg_ref[...] = norm_back(d_normed * ng_ref[...], hat_s[...], inv_s[...])

    spread_start(2)

    for side in range(2):
        along(lambda spot, side=side: line_copy(side, spot).wait_send())
        if B > 1:
            loop(0, A, lambda spot, side=side: lane_copy(side, spot).wait_send())
    for t in range(1, Q):
        other = wrap(q + t, Q)
        remote(tri_s.at[other], tri_rcv.at[q], tri_ss.at[t], tri_rs.at[q], r, other).wait_send()
        remote(drow.at[q], drow.at[q], drow_ss.at[t], drow_rs.at[q], r, other).wait_send()
    each_target(lambda b, t, target, other: col_copy(b, t, target, other).wait_send())
    for g in range(3):
        scatter_all(g).wait_send()
        spread_all(g).wait_recv()
    gall_ref[...] = gfin[...]
    for g in range(3):
        spread_all(g).wait_send()


def finish(NP, piece, C, H, block_ref, grad_ref, gall_ref, out_ref, pg_ref, gp_ref, gg_ref, go_ref):
    out_ref[...] = block_ref[...]
    pg_ref[...] = grad_ref[...]
    targets = (
        (gg_ref, 0), (go_ref, 0), (gp_ref, 0), (gp_ref, H), (gp_ref, 2 * H), (gp_ref, 3 * H),
    )
    per = C // piece
    for t, (ref, col) in enumerate(targets):
        for p in range(per):
            whole = (t % 2) * per + p
            ref[p * piece : (p + 1) * piece, col : col + H] = gall_ref[t // 2, whole].astype(F32)


def local(R, Q, pair_rep, cotangent, ng, nb, pw, gw, tg, tb, ow):
    rows, K, C = pair_rep.shape
    H = tg.shape[0]
    M = rows * K
    NP = R * Q
    RPQ = R // Q
    pad = -(-rows // 8) * 8
    piece = 2 * C // NP
    dma = pltpu.SemaphoreType.DMA
    vmem = pltpu.VMEM
    spec = pl.BlockSpec(memory_space=pltpu.VMEM)
    shapes = (
        jax.ShapeDtypeStruct((M, C), BF16),
        jax.ShapeDtypeStruct((M, C), F32),
        jax.ShapeDtypeStruct((3, NP, piece, H), BF16),
    )
    parts = pl.pallas_call(
        functools.partial(kernel, R, Q, rows, K, H, C),
        out_shape=shapes,
        in_specs=[spec] * 9,
        out_specs=[spec] * 3,
        scratch_shapes=[
            vmem((2, R, M, H), BF16),
            vmem((R * M, H), F32),
            vmem((R * M, H), F32),
            vmem((4, M, H), F32),
            vmem((M, C), F32),
            vmem((M, C), F32),
            vmem((M, C), F32),
            vmem((M, C), BF16),
            vmem((M, C), BF16),
            vmem((M, H), F32),
            vmem((Q, M, H), F32),
            vmem((Q, M, H), F32),
            vmem((M, H), F32),
            vmem((Q, M, H), BF16),
            vmem((Q * M, H), F32),
            vmem((RPQ, rows * pad, H), BF16),
            vmem((R, rows * pad, H), BF16),
            vmem((R * rows * pad, H), F32),
            vmem((M, H), BF16),
            vmem((M, C), BF16),
            vmem((3, NP, piece, H), BF16),
            vmem((3, NP, piece, H), BF16),
            vmem((3, NP, piece, H), BF16),
            dma((2, 2 * R)), dma((2, R)),
            dma((Q,)), dma((Q,)),
            dma((Q,)), dma((Q,)),
            dma((R,)), dma((R,)),
            dma((3,)), dma((3,)),
            dma((3,)), dma((3,)),
        ],
        compiler_params=pltpu.CompilerParams(
            collective_id=0, has_side_effects=True, vmem_limit_bytes=60 * 1024 * 1024
        ),
        name="triangle_step",
    )(
        pair_rep.reshape(M, C), cotangent.reshape(M, C), ng.reshape(1, C), nb.reshape(1, C),
        pw, gw, tg.reshape(1, H), tb.reshape(1, H), ow,
    )
    outs = pl.pallas_call(
        functools.partial(finish, NP, piece, C, H),
        out_shape=(
            shapes[0],
            shapes[1],
            jax.ShapeDtypeStruct((C, 4 * H), F32),
            jax.ShapeDtypeStruct((C, C), F32),
            jax.ShapeDtypeStruct((H, C), F32),
        ),
        in_specs=[spec] * 3,
        out_specs=[spec] * 5,
        name="finish",
    )(*parts)
    return (
        outs[0].reshape(rows, K, C), outs[1].reshape(rows, K, C), outs[2], outs[3], outs[4],
    )


def solution(mesh):
    tile = P(("crop", "row"), "col", None)
    grad = P("crop", None)
    return jax.shard_map(
        functools.partial(local, mesh.shape["row"], mesh.shape["col"]),
        mesh=mesh,
        in_specs=(tile, tile, P(), P(), P(), P(), P(), P(), P()),
        out_specs=(tile, tile, grad, grad, grad),
        check_vma=False,
    )
```

```python
import functools

import jax
import jax.numpy as jnp
from jax import lax
from jax.experimental import pallas as pl
from jax.experimental.pallas import tpu as pltpu
from jax.sharding import PartitionSpec as P

F32 = jnp.float32
BF16 = jnp.bfloat16


def mean_last(values):
    return jnp.mean(values, axis=-1, keepdims=True)


def normalise(values):
    centred = values - mean_last(values)
    inverse = lax.rsqrt(mean_last(centred * centred) + 1e-05)
    return centred * inverse, inverse


def norm_back(weighted, scaled, inverse):
    return inverse * (weighted - mean_last(weighted) - scaled * mean_last(weighted * scaled))


def dot(a, b, ca=1, cb=0):
    return lax.dot_general(a, b, (((ca,), (cb,)), ((), ())), preferred_element_type=F32)


def kernel(
    R, Q, rows, K, H, C,
    x_ref, cot_ref, ng_ref, nb_ref, pw_ref, gw_ref, tg_ref, tb_ref, ow_ref,
    out_ref, pg_ref, gall_ref,
    edges, right32, left32, coef, og_s, hat_s, inv_s, normed_s, dupd_s, dnorm_s,
    tri_s, tri_rcv, d32, drow, drow32, dsend, drecv, dcol32, tnorm_s, dgate_s,
    gsend, grecv, gfin,
    edge_ss, edge_rs, tri_ss, tri_rs, drow_ss, drow_rs, dcol_ss, dcol_rs,
    gs_ss, gs_rs, gf_ss, gf_rs,
):
    r = lax.axis_index("row")
    q = lax.axis_index("col")
    M = rows * K
    N = rows * R
    NP = R * Q
    RPQ = R // Q
    pad = -(-rows // 8) * 8
    me = r * Q + q

    def remote(src, dst, ss, rs, rr, qq):
        return pltpu.make_async_remote_copy(
            src_ref=src, dst_ref=dst, send_sem=ss, recv_sem=rs,
            device_id={"row": rr, "col": qq}, device_id_type=pl.DeviceIdType.MESH,
        )

    def loop(lo, hi, body):
        if hi - lo <= 16:
            for t in range(lo, hi):
                body(t)
            return

        def step(t, carry):
            body(t)
            return carry
        lax.fori_loop(lo, hi, step, 0)

    def wrap(value, size):
        return jnp.where(value >= size, value - size, value)

    def peer(t):
        rr, qq = wrap(r + t // Q, R), wrap(q + t % Q, Q)
        return rr, qq, rr * Q + qq

    barrier = pltpu.get_barrier_semaphore()

    def greet(t):
        rr, qq, _ = peer(t)
        pl.semaphore_signal(
            barrier, inc=1,
            device_id={"row": rr, "col": qq},
            device_id_type=pl.DeviceIdType.MESH,
        )

    loop(1, NP, greet)

    piece = 2 * C // NP
    per = NP // 2

    def scatter(g, t):
        rr, qq, other = peer(t)
        return remote(
            gsend.at[g, other], grecv.at[g, me], gs_ss.at[g], gs_rs.at[g], rr, qq
        )

    def scatter_all(g):
        block = pl.ds(0, NP - 1)
        return remote(
            gsend.at[g, block], grecv.at[g, block], gs_ss.at[g], gs_rs.at[g], r, q
        )

    def scatter_start(g, first, second):
        for p in range(per):
            gsend[g, p] = first[p * piece : (p + 1) * piece, :].astype(BF16)
            gsend[g, per + p] = second[p * piece : (p + 1) * piece, :].astype(BF16)
        loop(1, NP, lambda t: scatter(g, t).start())
        grecv[g, me] = gsend[g, me]

    def spread(g, t):
        rr, qq, _ = peer(t)
        return remote(gfin.at[g, me], gfin.at[g, me], gf_ss.at[g], gf_rs.at[g], rr, qq)

    def spread_all(g):
        block = pl.ds(0, NP - 1)
        return remote(gfin.at[g, block], gfin.at[g, block], gf_ss.at[g], gf_rs.at[g], r, q)

    def spread_start(g):
        scatter_all(g).wait_recv()
        total = grecv[g, 0].astype(F32)
        for p in range(1, NP):
            total = total + grecv[g, p].astype(F32)
        gfin[g, me] = (total / N).astype(BF16)
        loop(1, NP, lambda t: spread(g, t).start())

    hat, inv = normalise(x_ref[...].astype(F32))
    normed = (hat * ng_ref[...] + nb_ref[...]).astype(BF16)
    hat_s[...] = hat
    inv_s[...] = jnp.broadcast_to(inv, hat.shape)
    normed_s[...] = normed
    right = dot(normed, pw_ref[:, 2 * H :])
    sr = jax.nn.sigmoid(right[:, :H])
    vr = right[:, H:]
    right_edge = (sr * vr).astype(BF16)
    edges[0, r] = right_edge
    left = dot(normed, pw_ref[:, : 2 * H])
    sl = jax.nn.sigmoid(left[:, :H])
    vl = left[:, H:]
    left_edge = (sl * vl).astype(BF16)
    edges[1, r] = left_edge

    pl.semaphore_wait(barrier, NP - 1)

    B = 2 if R % 2 == 0 else 1
    A = R // B
    place, lane = r // B, lax.rem(r, B)

    def along(act):
        for d in range(1, A):
            for spot in (place - d, place + d):
                @pl.when(jnp.logical_and(spot >= 0, spot < A))
                def _(spot=spot):
                    act(jnp.clip(spot, 0, A - 1))

    def line_copy(side, spot):
        return remote(
            edges.at[side, r], edges.at[side, r], edge_ss.at[side, spot],
            edge_rs.at[side, r], spot * B + lane, q,
        )

    def lane_copy(side, spot):
        slot = spot * B + lane
        return remote(
            edges.at[side, slot], edges.at[side, slot], edge_ss.at[side, A + spot],
            edge_rs.at[side, slot], place * B + (B - 1 - lane), q,
        )

    def edge_send(side):
        along(lambda spot: line_copy(side, spot).start())
        if B > 1:
            lane_copy(side, place).start()

    def edge_pass(side):
        def one(spot):
            slot = spot * B + lane
            remote(
                edges.at[side, r], edges.at[side, slot], edge_ss.at[side, 0],
                edge_rs.at[side, slot], slot, q,
            ).wait_recv()
            if B > 1:
                lane_copy(side, spot).start()
        along(one)

    def edge_wait(side):
        if B > 1:
            def wait(spot):
                slot = spot * B + (B - 1 - lane)
                remote(
                    edges.at[side, r], edges.at[side, slot], edge_ss.at[side, 0],
                    edge_rs.at[side, slot], place * B + (B - 1 - lane), q,
                ).wait_recv()
            loop(0, A, wait)

    edge_send(0)

    own = pl.multiple_of(r * M, 8)
    left32[pl.ds(own, M), :] = left_edge.astype(F32)
    coef[0] = vl * sl * (1.0 - sl)
    coef[1] = sl
    coef[2] = vr * sr * (1.0 - sr)
    coef[3] = sr
    og = jax.nn.sigmoid(dot(normed, gw_ref[...]))
    og_s[...] = og
    d_update = (cot_ref[...].astype(F32) * og).astype(BF16)
    dupd_s[...] = d_update
    dnorm_s[...] = dot(d_update, ow_ref[...], 1, 1) * tg_ref[...]

    edge_pass(0)
    edge_send(1)
    edge_wait(0)

    def widen_right(t):
        right32[pl.ds(pl.multiple_of(t * M, 8), M), :] = edges[0, t].astype(F32)
    loop(0, R, widen_right)

    def partial(half):
        base = half * (K * K)

        def step(k, accs):
            block = right32[pl.ds(base + k, K, stride=K), :]
            return tuple(
                accs[i] + left32[pl.ds(own + i * K + k, 1), :] * block for i in range(rows)
            )
        accs = lax.fori_loop(
            0, K, step, tuple(jnp.zeros((K, H), F32) for _ in range(rows)), unroll=4
        )
        for i in range(rows):
            tri_s[half, i * K : (i + 1) * K, :] = accs[i]

    for t in range(1, Q):
        other = wrap(q + t, Q)
        partial(other)
        remote(
            tri_s.at[other], tri_rcv.at[q], tri_ss.at[t], tri_rs.at[q], r, other
        ).start()
    partial(q)
    edge_pass(1)
    triangle = tri_s[q]
    for t in range(1, Q):
        other = wrap(q + Q - t, Q)
        remote(
            tri_s.at[other], tri_rcv.at[other], tri_ss.at[t], tri_rs.at[other], r, other
        ).wait_recv()
        triangle = triangle + tri_rcv[other]

    tri_hat, tri_inv = normalise(triangle)
    d_tri = norm_back(dnorm_s[...], tri_hat, tri_inv).astype(BF16)
    drow[q] = d_tri
    for t in range(1, Q):
        other = wrap(q + t, Q)
        remote(drow.at[q], drow.at[q], drow_ss.at[t], drow_rs.at[q], r, other).start()
    d_tri32 = d_tri.astype(F32)
    d32[...] = d_tri32
    for b in range(RPQ):
        parts = []
        for i in range(rows):
            block = d32[i * K + b * rows : i * K + (b + 1) * rows, :]
            if pad > rows:
                block = jnp.concatenate([block, jnp.zeros((pad - rows, H), F32)], axis=0)
            parts.append(block)
        dsend[b] = jnp.concatenate(parts, axis=0).astype(BF16)

    def each_target(act):
        for t in range(Q):
            def one(b, t=t):
                target = q * RPQ + b
                other = wrap(q + t, Q)
                if t:
                    act(b, t, target, other)
                else:
                    @pl.when(target != r)
                    def _():
                        act(b, t, target, other)
            loop(0, RPQ, one)

    def col_copy(b, t, target, other):
        return remote(
            dsend.at[b], drecv.at[r], dcol_ss.at[t * RPQ + b], dcol_rs.at[r], target, other
        )

    each_target(lambda b, t, target, other: col_copy(b, t, target, other).start())
    mine = r // RPQ == q

    @pl.when(mine)
    def _():
        drecv[r] = dsend[lax.rem(r, RPQ)]

    tri_norm = (tri_hat * tg_ref[...] + tb_ref[...]).astype(BF16)
    update = dot(tri_norm, ow_ref[...])
    og = og_s[...]
    out_ref[...] = (og * update).astype(BF16)
    d_gate = (cot_ref[...].astype(F32) * update * og * (1.0 - og)).astype(BF16)
    dgate_s[...] = d_gate

    drow32[pl.ds(pl.multiple_of(q * M, 8), M), :] = d_tri32
    for t in range(1, Q):
        other = wrap(q + Q - t, Q)
        remote(
            drow.at[q], drow.at[other], drow_ss.at[t], drow_rs.at[other], r, other
        ).wait_recv()
        drow32[pl.ds(pl.multiple_of(other * M, 8), M), :] = drow[other].astype(F32)

    def zeros():
        return tuple(jnp.zeros((K, H), F32) for _ in range(rows))

    accs = zeros()
    for h in range(Q):
        def left_step(j, accs, h=h):
            block = right32[pl.ds(pl.multiple_of((h * K + j) * K, 8), K), :]
            return tuple(
                accs[i] + drow32[pl.ds(h * M + i * K + j, 1), :] * block for i in range(rows)
            )
        accs = lax.fori_loop(0, K, left_step, accs, unroll=4)
    d_left = jnp.concatenate(accs, axis=0)
    d_proj = [(d_left * coef[0]).astype(BF16), (d_left * coef[1]).astype(BF16)]
    wide = dot(normed_s[...], jnp.concatenate(d_proj, axis=-1), 0, 0)
    scatter_start(1, wide[:, :H], wide[:, H:])

    scatter_start(0, dot(normed_s[...], d_gate, 0, 0), dot(tri_norm, dupd_s[...], 0, 0))
    edge_wait(1)

    def widen_left(t):
        left32[pl.ds(pl.multiple_of(t * M, 8), M), :] = edges[1, t].astype(F32)
    loop(0, R, widen_left)

    owner = r // RPQ

    def col_wait(t):
        source = wrap(r + R - t, R)
        remote(
            dsend.at[0], drecv.at[source], dcol_ss.at[0], dcol_rs.at[source], source, owner
        ).wait_recv()
    loop(1, R, col_wait)

    @pl.when(jnp.logical_not(mine))
    def _():
        remote(dsend.at[0], drecv.at[r], dcol_ss.at[0], dcol_rs.at[r], r, owner).wait_recv()

    def widen_col(t):
        dcol32[pl.ds(pl.multiple_of(t * rows * pad, 8), rows * pad), :] = drecv[t].astype(F32)
    loop(0, R, widen_col)

    def right_step(i, accs):
        block = left32[pl.ds(pl.multiple_of(i * K, 8), K), :]
        return tuple(
            accs[j] + dcol32[pl.ds(i * pad + j, 1), :] * block for j in range(rows)
        )
    d_right = jnp.concatenate(lax.fori_loop(0, N, right_step, zeros(), unroll=4), axis=0)
    d_proj += [(d_right * coef[2]).astype(BF16), (d_right * coef[3]).astype(BF16)]

    wide = dot(normed_s[...], jnp.concatenate(d_proj[2:], axis=-1), 0, 0)
    scatter_start(2, wide[:, :H], wide[:, H:])
    spread_start(0)
    spread_start(1)

    d_cat = jnp.concatenate(d_proj, axis=-1)
    d_normed = dot(d_cat, pw_ref[...], 1, 1) + dot(dgate_s[...], gw_ref[...], 1, 1)
    pg_ref[...] = norm_back(d_normed * ng_ref[...], hat_s[...], inv_s[...])

    spread_start(2)

    for side in range(2):
        along(lambda spot, side=side: line_copy(side, spot).wait_send())
        if B > 1:
            loop(0, A, lambda spot, side=side: lane_copy(side, spot).wait_send())
    for t in range(1, Q):
        other = wrap(q + t, Q)
        remote(tri_s.at[other], tri_rcv.at[q], tri_ss.at[t], tri_rs.at[q], r, other).wait_send()
        remote(drow.at[q], drow.at[q], drow_ss.at[t], drow_rs.at[q], r, other).wait_send()
    each_target(lambda b, t, target, other: col_copy(b, t, target, other).wait_send())
    for g in range(3):
        scatter_all(g).wait_send()
        spread_all(g).wait_recv()
    gall_ref[...] = gfin[...]
    for g in range(3):
        spread_all(g).wait_send()


def finish(NP, piece, C, H, block_ref, grad_ref, gall_ref, out_ref, pg_ref, gp_ref, gg_ref, go_ref):
    out_ref[...] = block_ref[...]
    pg_ref[...] = grad_ref[...]
    targets = (
        (gg_ref, 0), (go_ref, 0), (gp_ref, 0), (gp_ref, H), (gp_ref, 2 * H), (gp_ref, 3 * H),
    )
    per = C // piece
    for t, (ref, col) in enumerate(targets):
        for p in range(per):
            whole = (t % 2) * per + p
            ref[p * piece : (p + 1) * piece, col : col + H] = gall_ref[t // 2, whole].astype(F32)


def local(R, Q, pair_rep, cotangent, ng, nb, pw, gw, tg, tb, ow):
    rows, K, C = pair_rep.shape
    H = tg.shape[0]
    M = rows * K
    NP = R * Q
    RPQ = R // Q
    pad = -(-rows // 8) * 8
    piece = 2 * C // NP
    dma = pltpu.SemaphoreType.DMA
    vmem = pltpu.VMEM
    spec = pl.BlockSpec(memory_space=pltpu.VMEM)
    shapes = (
        jax.ShapeDtypeStruct((M, C), BF16),
        jax.ShapeDtypeStruct((M, C), F32),
        jax.ShapeDtypeStruct((3, NP, piece, H), BF16),
    )
    parts = pl.pallas_call(
        functools.partial(kernel, R, Q, rows, K, H, C),
        out_shape=shapes,
        in_specs=[spec] * 9,
        out_specs=[spec] * 3,
        scratch_shapes=[
            vmem((2, R, M, H), BF16),
            vmem((R * M, H), F32),
            vmem((R * M, H), F32),
            vmem((4, M, H), F32),
            vmem((M, C), F32),
            vmem((M, C), F32),
            vmem((M, C), F32),
            vmem((M, C), BF16),
            vmem((M, C), BF16),
            vmem((M, H), F32),
            vmem((Q, M, H), F32),
            vmem((Q, M, H), F32),
            vmem((M, H), F32),
            vmem((Q, M, H), BF16),
            vmem((Q * M, H), F32),
            vmem((RPQ, rows * pad, H), BF16),
            vmem((R, rows * pad, H), BF16),
            vmem((R * rows * pad, H), F32),
            vmem((M, H), BF16),
            vmem((M, C), BF16),
            vmem((3, NP, piece, H), BF16),
            vmem((3, NP, piece, H), BF16),
            vmem((3, NP, piece, H), BF16),
            dma((2, 2 * R)), dma((2, R)),
            dma((Q,)), dma((Q,)),
            dma((Q,)), dma((Q,)),
            dma((R,)), dma((R,)),
            dma((3,)), dma((3,)),
            dma((3,)), dma((3,)),
        ],
        compiler_params=pltpu.CompilerParams(
            collective_id=0, has_side_effects=True, vmem_limit_bytes=60 * 1024 * 1024
        ),
        name="triangle_step",
    )(
        pair_rep.reshape(M, C), cotangent.reshape(M, C), ng.reshape(1, C), nb.reshape(1, C),
        pw, gw, tg.reshape(1, H), tb.reshape(1, H), ow,
    )
    outs = pl.pallas_call(
        functools.partial(finish, NP, piece, C, H),
        out_shape=(
            shapes[0],
            shapes[1],
            jax.ShapeDtypeStruct((C, 4 * H), F32),
            jax.ShapeDtypeStruct((C, C), F32),
            jax.ShapeDtypeStruct((H, C), F32),
        ),
        in_specs=[spec] * 3,
        out_specs=[spec] * 5,
        name="finish",
    )(*parts)
    return (
        outs[0].reshape(rows, K, C), outs[1].reshape(rows, K, C), outs[2], outs[3], outs[4],
    )


def solution(mesh):
    tile = P(("crop", "row"), "col", None)
    grad = P("crop", None)
    return jax.shard_map(
        functools.partial(local, mesh.shape["row"], mesh.shape["col"]),
        mesh=mesh,
        in_specs=(tile, tile, P(), P(), P(), P(), P(), P(), P()),
        out_specs=(tile, tile, grad, grad, grad),
        check_vma=False,
    )
```
